512 devices in a mesh: rows: 32 (over z, x), cols: 16 (over y, core).
Axes of the slice: x: 4, y: 8, z: 8, core: 2. Of those that a mesh axis runs over, the one named last changes fastest.
Arguments:
- tokens: bfloat16 [8192, 4096], P('rows', 'cols'), may hold values from -6 to 6
- cotangent: bfloat16 [8192, 4096], P('rows', 'cols'), may hold values from -6 to 6
- gate_weight: bfloat16 [4096, 7168], P('rows', 'cols'), may hold values from -0.09375 to 0.09375
- down_weight: bfloat16 [4096, 7168], P('rows', 'cols'), may hold values from -0.0625 to 0.0625
- proj_in: bfloat16 [4096, 128], replicated, may hold values from -0.09375 to 0.09375
- proj_out: bfloat16 [7168, 64], P('cols'), may hold values from -0.0625 to 0.0625
- lengths: int32 [128], P('rows'), may hold values from 16 to 64
- loss_mask: int32 [128, 64], P('rows'), may hold values 0 or 1
- gram_in: float32 [8, 1024, 8, 1024], P(None, 'rows', None, 'cols'), as said below
- queries: float32 [256, 8, 1024], P('cols', None, 'rows'), may hold values from -6 to 6
Outputs:
- gram_next: float32 [8, 1024, 8, 1024], P(None, 'rows', None, 'cols')
- query_next: float32 [256, 8, 1024], P('cols', None, 'rows')
- scores: float32 [256, 128], P('cols', 'rows')
The draws below stay inside these ranges and needn't reach their ends.
Inputs may be any that keep to these rules, and one draw needn't show every extreme that they name: gram_in, read as a 8192 x 8192 matrix, is symmetric positive definite.
All inputs are finite; a program needn't handle non-finite values. No bound on the sum of `loss_mask` on one device may be relied on, other than what follows from the above.
Results may differ from the reference program's by a relative error of at most 0.004.
Values may be sent and summed in bfloat16 or wider, within the bound.
A program may use at most 128 MiB of HBM per device.

```python
import math
import jax
import jax.numpy as jnp
from jax import lax

D = 4096
FF_WIN = 7168
K_IN = 128
K_OUT = 64
WIN = 64
PW = 1024
QN = 256
SEQS = 128
TOKENS = 8192
FEAT = 8192
CYC = 8


def draw_gram_in(key, part):
    key_noise, key_diag = jax.random.split(key, 2)
    noise_raw = jax.random.normal(key_noise, (FEAT, FEAT), jnp.float32)
    matrix = (noise_raw + noise_raw.T) * (0.6 / math.sqrt(FEAT))
    diagonal = jnp.exp(jax.random.uniform(key_diag, (FEAT,), jnp.float32, math.log(2.5), math.log(10.0)))
    matrix = matrix + jnp.diag(diagonal)
    return matrix.reshape(CYC, PW, CYC, PW)


def set_ends(values, stream_key, least, largest):
    longest = values.shape.index(max(values.shape))
    spots = []
    for shift in (0, 1):
        where = [jax.random.randint(jax.random.fold_in(stream_key, axis), (), 0, length) for axis, length in enumerate(values.shape)]
        where[longest] = (where[longest] + shift) % values.shape[longest]
        spots.append(tuple(where))
    return values.at[spots[0]].set(least).at[spots[1]].set(largest)


def levels(own_key, dims, cuts, least, largest):
    def one(axis_at, blocks):
        steps = jax.random.uniform(jax.random.fold_in(jax.random.fold_in(own_key, 6), axis_at), (blocks,), jnp.float32, least / len(cuts), largest / len(cuts))
        return jnp.repeat(jnp.exp(steps), dims[axis_at] // blocks).reshape((-1,) + (1,) * (len(dims) - axis_at - 1))

    factor_of = one(*cuts[0])
    for cut in cuts[1:]:
        factor_of = factor_of * one(*cut)
    return factor_of


def noise(rng, dims, scale, limit, cuts=(), kind=jnp.bfloat16):
    values = jax.random.normal(rng, dims, jnp.float32) * scale
    if len(cuts) > 0:
        values = levels(rng, dims, cuts, -0.22, 0.18) * values
    return jnp.clip(values, min=-limit, max=limit).astype(kind)


def setup_inputs(seed: int = 0) -> dict:
    keys = jax.random.split(jax.random.key(seed), 11)
    return {
        "tokens": noise(keys[0], (TOKENS, D), 1.0, 6.0, ((0, 32), (1, 16))),
        "cotangent": noise(keys[1], (TOKENS, D), 1.0, 6.0, ((0, 32), (1, 16))),
        "gate_weight": noise(keys[2], (D, FF_WIN), D ** -0.5, 0.09375, ((0, 32), (1, 16))),
        "down_weight": noise(keys[3], (D, FF_WIN), FF_WIN ** -0.5, 0.0625, ((0, 32), (1, 16))),
        "proj_in": noise(keys[4], (D, K_IN), D ** -0.5, 0.09375),
        "proj_out": noise(keys[5], (FF_WIN, K_OUT), FF_WIN ** -0.5, 0.0625, ((0, 16),)),
        "lengths": set_ends(jax.random.randint(keys[6], (SEQS,), WIN // 4, WIN + 1), jax.random.fold_in(keys[6], 1), WIN // 4, WIN).astype(jnp.int32),
        "loss_mask": set_ends((jax.random.randint(keys[7], (SEQS, WIN), 0, 4) < 3).astype(jnp.int32), jax.random.fold_in(keys[7], 1), 0, 1),
        "gram_in": draw_gram_in(jax.random.fold_in(keys[10], 71), 0),
        "queries": noise(keys[9], (QN, CYC, PW), 1.0, 6.0, ((0, 16), (2, 32)), jnp.float32),
    }


highest = lax.Precision.HIGHEST

def reference(tokens, cotangent, gate_weight, down_weight, proj_in, proj_out, lengths, loss_mask, gram_in, queries):
    gate_pre = jnp.dot(tokens.astype(jnp.float32), gate_weight.astype(jnp.float32), preferred_element_type=jnp.float32)
    grad_hidden = jnp.dot(cotangent.astype(jnp.float32), down_weight.astype(jnp.float32), preferred_element_type=jnp.float32)
    grad_up = (grad_hidden * jax.nn.silu(gate_pre)).astype(jnp.bfloat16)
    proj_inner = jnp.dot(tokens.astype(jnp.float32), proj_in.astype(jnp.float32), preferred_element_type=jnp.float32)
    proj_outer = jnp.dot(grad_up.astype(jnp.float32), proj_out.astype(jnp.float32), preferred_element_type=jnp.float32)
    positions = jnp.arange(WIN, dtype=jnp.int32)
    token_live = (positions[None, :] >= (WIN - lengths)[:, None]).astype(jnp.float32) * loss_mask.astype(jnp.float32)
    weighted = proj_inner.reshape(SEQS, WIN, K_IN) * token_live[:, :, None]
    features = jnp.einsum('stk,stl->skl', weighted, proj_outer.reshape(SEQS, WIN, K_OUT), precision=highest)
    features = features.reshape(SEQS, FEAT)
    updated = gram_in.reshape(FEAT, FEAT) + jnp.dot(features.T.astype(jnp.float32), features.astype(jnp.float32), precision=highest, preferred_element_type=jnp.float32) / SEQS
    factor = jnp.linalg.cholesky(updated[:PW, :PW])
    lower_part = jax.scipy.linalg.solve_triangular(factor, updated[PW:, :PW].T, lower=True).T
    panel_cols = jnp.concatenate([factor, lower_part], axis=0)
    gram_next = updated.at[:, :PW].set(panel_cols).reshape(CYC, PW, CYC, PW)
    query_flat = queries.reshape(QN, FEAT)
    solved = jax.scipy.linalg.solve_triangular(factor, query_flat[:, :PW].T, lower=True)
    query_tail = query_flat[:, PW:] - jnp.dot(solved.T.astype(jnp.float32), lower_part.T.astype(jnp.float32), precision=highest, preferred_element_type=jnp.float32)
    query_next = jnp.concatenate([solved.T, query_tail], axis=1).reshape(QN, CYC, PW)
    whitened = jax.scipy.linalg.solve_triangular(factor, features[:, :PW].T, lower=True)
    scores = jnp.dot(solved.T.astype(jnp.float32), whitened.astype(jnp.float32), precision=highest, preferred_element_type=jnp.float32)
    return (gram_next, query_next, scores)
```

```python
import jax
import jax.numpy as jnp
from jax import lax
from jax.experimental import pallas as pl
from jax.experimental.pallas import tpu as pltpu
from jax.sharding import PartitionSpec as P

HI = lax.Precision.HIGHEST
NB = 128

NZ, NX, NY, NC = 8, 4, 8, 2
DIMS = (NZ, NX, NY, NC)
MESH = pl.DeviceIdType.MESH


def add(a, b):
    return tuple((p + q) % n for p, q, n in zip(a, b, DIMS))


def neg(a):
    return tuple((-p) % n for p, n in zip(a, DIMS))


class Msg:
    def __init__(self, array, part, origin, off, dep, size):
        self.array, self.part, self.origin, self.off, self.dep, self.size = array, part, origin, off, dep, size


def ring(msgs, array, part, axis, start, dep, size, plus, minus):
    arrivals = []
    for step, hops in ((1, plus), (-1, minus)):
        unit = tuple(step if a == axis else 0 for a in range(4))
        unit = tuple(u % n for u, n in zip(unit, DIMS))
        origin, last = start, dep
        for _ in range(hops):
            m = Msg(array, part, origin, unit, last, size)
            msgs.append(m)
            origin = add(origin, neg(unit))
            arrivals.append((origin, m))
            last = m
    return arrivals


def ordered(msgs):
    import heapq
    free, done, pending = {}, {}, []
    followers = {}
    for n, m in enumerate(msgs):
        if m.dep is None:
            heapq.heappush(pending, (0.0, n))
        else:
            followers.setdefault(id(m.dep), []).append(n)
    while pending:
        at, n = heapq.heappop(pending)
        m = msgs[n]
        near = m.off == (0, 0, 0, 1)
        rate, hop = (250e3, 0.9) if near else (45e3, 1.7)
        begin = max(at, free.get(m.off, 0.0))
        free[m.off] = begin + m.size / rate
        done[n] = free[m.off] + hop
        for f in followers.get(id(m), []):
            heapq.heappush(pending, (done[n], f))
    return done


def position():
    r, c = lax.axis_index("rows"), lax.axis_index("cols")
    return (r // NX, lax.rem(r, NX), c // NC, lax.rem(c, NC))


def moved(me, off):
    return tuple(p if o == 0 else lax.rem(p + o, n) for p, o, n in zip(me, off, DIMS))


def device(me, off):
    z, x, y, k = moved(me, off)
    return {"rows": z * NX + x, "cols": y * NC + k}


def greet(me, offs):
    both = sorted(set(offs) | set(neg(o) for o in offs))
    barrier = pltpu.get_barrier_semaphore()
    for o in both:
        pl.semaphore_signal(barrier, inc=1, device_id=device(me, o), device_id_type=MESH)
    pl.semaphore_wait(barrier, len(both))


SPLIT = 80


def gather_messages(tsize, gsize, wrow, depth):
    msgs = []
    here = (0, 0, 0, 0)
    core = (0, 0, 0, 1)
    held = []
    for array, size, plus, minus in (("tok", tsize, 4, 3), ("cot", tsize, 3, 4), ("gp", gsize, 4, 3)):
        held += [(array, size, here, None)]
        held += [(array, size, o, m) for o, m in ring(msgs, array, 0, 2, here, None, size, plus, minus)]
    for array, size, o, m in held:
        msgs.append(Msg(array, 0, o, core, m, size))
    size = wrow * SPLIT
    got = [(here, None)] + ring(msgs, "w", 0, 0, here, None, size, 4, 3)
    for o, m in got:
        even = o[0] % 2 == 0
        ring(msgs, "w", 0, 1, o, m, size, 2 if even else 1, 1 if even else 2)
    size = wrow * (depth - SPLIT)
    got = [(here, None)] + ring(msgs, "w", 1, 1, here, None, size, 2, 1)
    for o, m in got:
        even = o[1] % 2 == 0
        ring(msgs, "w", 1, 0, o, m, size, 4 if even else 3, 3 if even else 4)
    return msgs


def gather_kernel(msgs, order, tok, cot, w, gp, tok_all, cot_all, w_all, gp_all, send, recv, own):
    me = position()
    depth, width, band = w.shape[0], tok.shape[1], gp.shape[0]

    def place(array, part, origin):
        z, x, y, k = moved(me, origin)
        if array == "w":
            at, rows = (0, SPLIT) if part == 0 else (SPLIT, depth - SPLIT)
            return w_all.at[pl.ds(pl.multiple_of((z * NX + x) * depth + at, 16), rows), :]
        c = y * NC + k
        if array == "gp":
            return gp_all.at[pl.ds(pl.multiple_of(c * band, 8), band), :]
        whole = tok_all if array == "tok" else cot_all
        return whole.at[:, pl.ds(pl.multiple_of(c * width, 128), width)]

    def mine(array, part):
        if array == "w":
            at, rows = (0, SPLIT) if part == 0 else (SPLIT, depth - SPLIT)
            return w.at[pl.ds(at, rows), :]
        return {"tok": tok, "cot": cot, "gp": gp}[array]

    def copy(n):
        m = msgs[n]
        src = mine(m.array, m.part) if m.origin == (0, 0, 0, 0) else place(m.array, m.part, m.origin)
        return pltpu.make_async_remote_copy(
            src_ref=src, dst_ref=place(m.array, m.part, m.origin), send_sem=send.at[n], recv_sem=recv.at[n],
            device_id=device(me, m.off), device_id_type=MESH)

    def arrived(n):
        m = msgs[n]
        there = place(m.array, m.part, add(m.origin, neg(m.off)))
        pltpu.make_async_remote_copy(
            src_ref=there, dst_ref=there, send_sem=send.at[n], recv_sem=recv.at[n],
            device_id=device(me, m.off), device_id_type=MESH).wait_recv()

    here = (0, 0, 0, 0)
    kept = [pltpu.make_async_copy(mine(a, p), place(a, p, here), own.at[i])
            for i, (a, p) in enumerate((("tok", 0), ("cot", 0), ("gp", 0), ("w", 0), ("w", 1)))]
    for c in kept:
        c.start()
    greet(me, [m.off for m in msgs])
    for n, m in enumerate(msgs):
        if m.dep is None:
            copy(n).start()
    for n in order:
        arrived(n)
        for f, m in enumerate(msgs):
            if m.dep is msgs[n]:
                copy(f).start()
    for n in range(len(msgs)):
        copy(n).wait_send()
    for c in kept:
        c.wait()


def gather(tok, cot, w, gp):
    msgs = gather_messages(tok.size * 2, gp.size * 4, w.shape[1] * 2, w.shape[0])
    times = ordered(msgs)
    order = sorted(range(len(msgs)), key=lambda n: (times[n], n))
    vm = pl.BlockSpec(memory_space=pltpu.VMEM)

    def body(*refs):
        gather_kernel(msgs, order, *refs)
    rows = NZ * NX
    cols = NY * NC
    return pl.pallas_call(
        body,
        out_shape=(
            jax.ShapeDtypeStruct((tok.shape[0], tok.shape[1] * cols), tok.dtype),
            jax.ShapeDtypeStruct((cot.shape[0], cot.shape[1] * cols), cot.dtype),
            jax.ShapeDtypeStruct((w.shape[0] * rows, w.shape[1]), w.dtype),
            jax.ShapeDtypeStruct((gp.shape[0] * cols, gp.shape[1]), gp.dtype)),
        in_specs=[vm] * 4, out_specs=(vm,) * 4,
        scratch_shapes=[pltpu.SemaphoreType.DMA((len(msgs),)), pltpu.SemaphoreType.DMA((len(msgs),)),
                        pltpu.SemaphoreType.DMA((5,))],
        compiler_params=pltpu.CompilerParams(collective_id=0, has_side_effects=True, vmem_limit_bytes=40 << 20),
        name="gather",
    )(tok, cot, w, gp)


def exchange_messages(size):
    msgs = []
    here = (0, 0, 0, 0)
    held = []
    got = [(here, None)] + ring(msgs, "d", 0, 0, here, None, size, 4, 3)
    for o, m in got:
        even = o[0] % 2 == 0
        held += [(0, o, m)] + [(0, p, q) for p, q in ring(msgs, "d", 0, 1, o, m, size, 2 if even else 1, 1 if even else 2)]
    got = [(here, None)] + ring(msgs, "d", 1, 1, here, None, size, 2, 1)
    for o, m in got:
        even = o[1] % 2 == 0
        held += [(1, o, m)] + [(1, p, q) for p, q in ring(msgs, "d", 1, 0, o, m, size, 4 if even else 3, 3 if even else 4)]
    for part, o, m in held:
        msgs.append(Msg("d", part, o, (0, 0, 0, 1), m, size))
    return msgs


HALF = 512
TAKE = 96
SUM_AT, SPREAD_AT, PANEL_AT = 8.0, 19.0, 27.0


def exchange_kernel(msgs, times, fp, dp, col_all, all3, d_all, d_other,
                    parts, hbuf, p3, dsend, drecv, s1, r1, s2, r2, sl, rl, s3, r3, s4, r4, own):
    me = position()
    r, c = lax.axis_index("rows"), lax.axis_index("cols")
    here, core = (0, 0, 0, 0), (0, 0, 0, 1)
    band = dp.shape[0]
    half = band // 2

    def rdma(src, dst, send, recv, to):
        return pltpu.make_async_remote_copy(src_ref=src, dst_ref=dst, send_sem=send, recv_sem=recv,
                                            device_id=to, device_id_type=MESH)

    def row_of(origin, part):
        z, x, _, _ = moved(me, origin)
        return pl.ds(pl.multiple_of((z * NX + x) * band + half * part, 8), half)

    def dcopy(n):
        m = msgs[n]
        src = dp.at[pl.ds(half * m.part, half), :] if m.origin == here else d_all.at[row_of(m.origin, m.part), :]
        if m.off == core:
            src = (dp.at[pl.ds(half * m.part, half), pl.ds(0, HALF)] if m.origin == here
                   else d_all.at[row_of(m.origin, m.part), pl.ds(0, HALF)])
            dst = d_other.at[row_of(m.origin, m.part), :]
        else:
            dst = d_all.at[row_of(m.origin, m.part), :]
        return rdma(src, dst, dsend.at[n], drecv.at[n], device(me, m.off))

    def darrived(n):
        m = msgs[n]
        if m.off == core:
            there = d_other.at[row_of(m.origin, m.part), :]
        else:
            there = d_all.at[row_of(add(m.origin, neg(m.off)), m.part), :]
        rdma(there, there, dsend.at[n], drecv.at[n], device(me, m.off)).wait_recv()

    cols_off = [(0, 0, dy, dk) for dy in range(NY) for dk in range(NC) if (dy, dk) != (0, 0)]
    rows_off = [(dz, dx, 0, 0) for dz in range(NZ) for dx in range(NX) if (dz, dx) != (0, 0)]
    y_off = [(0, 0, dy, 0) for dy in range(1, NY)]
    legs = [{"rows": 2 * c + e, "cols": r // 2} for e in range(2)]
    at_home = [jnp.logical_and(c == r // 2, lax.rem(r, 2) == e) for e in range(2)]

    def col_of(off):
        _, _, y, k = moved(me, off)
        return y * NC + k

    kept = pltpu.make_async_copy(dp, d_all.at[pl.ds(pl.multiple_of(r * band, 8), band), :], own)
    kept.start()
    both = sorted(set(cols_off + rows_off))
    barrier = pltpu.get_barrier_semaphore()
    for o in both:
        pl.semaphore_signal(barrier, inc=1, device_id=device(me, o), device_id_type=MESH)
    for e in range(2):
        @pl.when(jnp.logical_not(at_home[e]))
        def _():
            pl.semaphore_signal(barrier, inc=1, device_id=legs[e], device_id_type=MESH)
    pl.semaphore_wait(barrier, jnp.where(c == r // 2, len(both) + 1, len(both) + 2))

    first = [rdma(fp.at[col_of(o)], parts.at[i], s1.at[i], r1.at[i], device(me, o)) for i, o in enumerate(cols_off)]
    my_rows = pl.ds(pl.multiple_of(r * 16, 16), 16)
    second = [rdma(hbuf, col_all.at[my_rows, :], s2.at[i], r2.at[i], device(me, o)) for i, o in enumerate(rows_off)]
    leg_to = p3.at[pl.ds(pl.multiple_of(64 + lax.rem(r, 2) * 16, 16), 16), :]
    leg = [rdma(hbuf, leg_to, sl.at[e], rl.at[lax.rem(r, 2)], legs[e]) for e in range(2)]
    my_take = pl.ds(pl.multiple_of(c * TAKE, 8), TAKE)
    third = [rdma(p3, all3.at[my_take, :], s3.at[i], r3.at[i], device(me, o)) for i, o in enumerate(y_off)]

    def take_of(off):
        return all3.at[pl.ds(pl.multiple_of(col_of(off) * TAKE, 8), TAKE), :]

    def give(i):
        off = here if i == 0 else neg(y_off[i - 1])
        src = p3 if i == 0 else take_of(off)
        return rdma(src, take_of(off), s4.at[i], r4.at[i], device(me, core))

    def sum_up():
        total = fp[c]
        for i in range(len(cols_off)):
            first[i].wait_recv()
            total = total + parts[i]
        hbuf[...] = total
        col_all[my_rows, :] = total
        for e in range(2):
            @pl.when(jnp.logical_not(at_home[e]))
            def _():
                leg[e].start()

            @pl.when(at_home[e])
            def _():
                p3[pl.ds(64 + 16 * e, 16), :] = total
        for copy in second:
            copy.start()

    def spread():
        for i, o in enumerate(rows_off):
            z, x, _, _ = moved(me, neg(o))
            there = col_all.at[pl.ds(pl.multiple_of((z * NX + x) * 16, 16), 16), :]
            rdma(there, there, s2.at[i], r2.at[i], device(me, o)).wait_recv()
        for n in range(NZ * NX):
            p3[pl.ds(2 * n, 2), :] = col_all[pl.ds(16 * n, 2), :]
        for e in range(2):
            @pl.when(jnp.logical_not(at_home[e]))
            def _():
                there = p3.at[pl.ds(64 + 16 * e, 16), :]
                rdma(there, there, sl.at[e], rl.at[e], legs[e]).wait_recv()
        all3[my_take, :] = p3[...]
        for copy in third:
            copy.start()
        give(0).start()

    def panel():
        for i, o in enumerate(y_off):
            there = take_of(neg(o))
            rdma(there, there, s3.at[i], r3.at[i], device(me, o)).wait_recv()
            give(i + 1).start()

    for copy in first:
        copy.start()
    for n, m in enumerate(msgs):
        if m.dep is None:
            dcopy(n).start()
    events = sorted([(times[n], n) for n in range(len(msgs))]
                    + [(SUM_AT, -1), (SPREAD_AT, -2), (PANEL_AT, -3)])
    for _, n in events:
        if n < 0:
            (sum_up, spread, panel)[-n - 1]()
            continue
        darrived(n)
        for f, m in enumerate(msgs):
            if m.dep is msgs[n]:
                dcopy(f).start()
    for i in range(NY):
        off = here if i == 0 else neg(y_off[i - 1])
        there = take_of(add(off, core))
        rdma(there, there, s4.at[i], r4.at[i], device(me, core)).wait_recv()
    for n in range(len(msgs)):
        dcopy(n).wait_send()
    for copy in first + second + third:
        copy.wait_send()
    for e in range(2):
        @pl.when(jnp.logical_not(at_home[e]))
        def _():
            leg[e].wait_send()
    for i in range(NY):
        give(i).wait_send()
    kept.wait()


def exchange(fp, dp):
    msgs = exchange_messages(dp.size * 2)
    times = ordered(msgs)
    vm = pl.BlockSpec(memory_space=pltpu.VMEM)
    f32 = jnp.float32
    rows, cols = NZ * NX, NY * NC
    dma = pltpu.SemaphoreType.DMA

    def body(*refs):
        exchange_kernel(msgs, times, *refs)
    return pl.pallas_call(
        body,
        out_shape=(
            jax.ShapeDtypeStruct((rows * 16, 128), f32),
            jax.ShapeDtypeStruct((cols * TAKE, 128), f32),
            jax.ShapeDtypeStruct((rows * dp.shape[0], dp.shape[1]), f32),
            jax.ShapeDtypeStruct((rows * dp.shape[0], HALF), f32)),
        in_specs=[vm] * 2, out_specs=(vm,) * 4,
        scratch_shapes=[
            pltpu.VMEM((cols - 1, 16, 128), f32), pltpu.VMEM((16, 128), f32), pltpu.VMEM((TAKE, 128), f32),
            dma((len(msgs),)), dma((len(msgs),)), dma((cols - 1,)), dma((cols - 1,)), dma((rows - 1,)), dma((rows - 1,)),
            dma((2,)), dma((2,)), dma((NY - 1,)), dma((NY - 1,)), dma((NY,)), dma((NY,)), dma],
        compiler_params=pltpu.CompilerParams(collective_id=1, has_side_effects=True, vmem_limit_bytes=40 << 20),
        name="exchange",
    )(fp, dp)


def lanes(x, j):
    return jnp.broadcast_to(x[:, j:j + 1], x.shape)


def subl(x, k):
    return jnp.broadcast_to(x[k:k + 1, :], x.shape)


def factor_block(A, V):
    n = len(A)
    A = list(A); V = list(V)
    sub = lax.broadcasted_iota(jnp.int32, (8, NB), 0)
    for p in range(n):
        a, v = A[p], V[p]
        C = [lanes(a, 8 * p + j) for j in range(8)]
        Us, Vs, R, S = [], [], [], []
        for k in range(8):
            d = subl(C[k], k)
            r = lax.rsqrt(d)
            sb = [subl(C[k], j) if j > k else None for j in range(8)]
            rd = r * r
            Cs = C[k] * rd
            for j in range(k + 1, 8):
                C[j] = C[j] - Cs * sb[j]
            R.append(r)
            S.append([None if s is None else s * r for s in sb])
            uk = subl(a, k) * r
            vk = subl(v, k) * r
            m = jnp.where(sub > k, C[k] * r, 0.0)
            a = a - m * uk
            v = v - m * vk
            Us.append(uk); Vs.append(vk)
        un, vn = Us[0], Vs[0]
        for k in range(1, 8):
            un = jnp.where(sub == k, Us[k], un)
            vn = jnp.where(sub == k, Vs[k], vn)
        A[p], V[p] = un, vn
        for q in range(p + 1, n):
            aq, vq = A[q], V[q]
            if q == p + 1:
                G = [lanes(aq, 8 * p + j) for j in range(8)]
                L = []
                for k in range(8):
                    t = G[k]
                    for m in range(k):
                        t = t - L[m] * S[m][k]
                    L.append(t * R[k])
                for k in range(8):
                    aq = aq - L[k] * Us[k]
                    vq = vq - L[k] * Vs[k]
            else:
                for k in range(8):
                    l = lanes(aq, 8 * p + k) * R[k]
                    aq = aq - l * Us[k]
                    vq = vq - l * Vs[k]
            A[q], V[q] = aq, vq
    return A, V


def factor_kernel(x, y, gp, f0, frow, u_ref, inv_ref):
    n = u_ref.shape[0]
    nb = n // NB
    seqs = f0.shape[0]
    r = lax.axis_index("rows")
    k = lax.rem(lax.axis_index("cols"), NC)
    own = seqs // (NZ * NX)
    heads = 16
    lane = lax.broadcasted_iota(jnp.int32, (seqs, 256), 1)
    seq = lax.broadcasted_iota(jnp.int32, (seqs, 256), 0)
    pick = jnp.where(jnp.logical_and(lane >= heads, lane < heads + own), jnp.where(seq == own * r + lane - heads, 1.0, 0.0), 0.0)
    z = jnp.where(lane < 32, pick, frow[...] * (1.0 / seqs))
    row = lax.broadcasted_iota(jnp.int32, (8, NB), 0)
    col = lax.broadcasted_iota(jnp.int32, (8, NB), 1)
    tdot = lambda a, b: lax.dot_general(a, b, (((0,), (0,)), ((), ())), precision=HI, preferred_element_type=jnp.float32)

    for b in range(nb):
        rows = pl.ds(b * NB, NB)
        u_ref[rows, pl.ds(pl.multiple_of(k * HALF, HALF), HALF)] = x[rows, :HALF]
        u_ref[rows, pl.ds(pl.multiple_of((1 - k) * HALF, HALF), HALF)] = y[rows, :]
        lhs = f0[:, b * NB:(b + 1) * NB]
        u_ref[rows, :n] = u_ref[rows, :n] + tdot(lhs, f0[...]) * (1.0 / seqs)
        low = lane[:NB, :NB]
        base = jnp.where(low < heads, x[rows, HALF:], jnp.where(low < 32, 0.0, gp[rows, :NB]))
        extra = tdot(lhs, z)
        u_ref[rows, n:n + NB] = base + extra[:, :NB]
        u_ref[rows, n + NB:] = gp[rows, NB:] + extra[:, NB:]

    def outer(b, _):
        o = pl.multiple_of(b * NB, NB)
        A = [u_ref[pl.ds(o + 8 * p, 8), pl.ds(o, NB)] for p in range(16)]
        V = [jnp.where(col == row + 8 * p, 1.0, 0.0) for p in range(16)]
        A, V = factor_block(A, V)
        for p in range(16):
            inv_ref[pl.ds(8 * p, 8), :] = V[p]
        u_ref[pl.ds(o, NB), :] = jnp.dot(inv_ref[...], u_ref[pl.ds(o, NB), :], precision=HI, preferred_element_type=jnp.float32)
        for p in range(16):
            u_ref[pl.ds(o + 8 * p, 8), pl.ds(o, NB)] = jnp.where(col >= row + 8 * p, A[p], 0.0)

        def trail(q, _):
            oq = pl.multiple_of(q * NB, NB)
            lhs = u_ref[pl.ds(o, NB), pl.ds(oq, NB)]
            u_ref[pl.ds(oq, NB), :] = u_ref[pl.ds(oq, NB), :] - tdot(lhs, u_ref[pl.ds(o, NB), :])
            return 0
        lax.fori_loop(b + 1, nb, trail, 0)
        return 0
    lax.fori_loop(0, nb, outer, 0)


def factored(x, y, gp, f0, frow):
    n = x.shape[0]
    vm = pl.BlockSpec(memory_space=pltpu.VMEM)
    return pl.pallas_call(
        factor_kernel,
        out_shape=jax.ShapeDtypeStruct((n, n + 256), jnp.float32),
        in_specs=[vm] * 5, out_specs=vm,
        scratch_shapes=[pltpu.VMEM((NB, NB), jnp.float32)],
        compiler_params=pltpu.CompilerParams(vmem_limit_bytes=40 << 20),
        name="factor",
    )(x, y, gp, f0, frow)


def local(tokens, cotangent, gate_weight, down_weight, proj_in, proj_out, lengths, loss_mask, gram_in, queries):
    f32 = jnp.float32
    r, c = lax.axis_index("rows"), lax.axis_index("cols")
    k = lax.rem(c, NC)
    cycles, band_rows, _, band_cols = gram_in.shape
    seq_count, window = loss_mask.shape
    hidden = gate_weight.shape[1]
    rows, cols = NZ * NX, NY * NC
    seqs = seq_count * rows
    pw = band_rows * rows

    weights = jnp.concatenate([gate_weight, down_weight], axis=1)
    band = gram_in[:, :, 0, :].reshape(cycles * band_rows, band_cols).T
    tok, cot, wts, gp = gather(tokens, cotangent, weights, band)

    diag = gp[:, :band_rows].T
    diag = lax.dynamic_slice_in_dim(diag, k * HALF, HALF, 1)
    head = jnp.pad(queries[:, 0, :].T, ((0, 0), (0, 128 - queries.shape[0])))
    dp = jnp.concatenate([diag, head], axis=1)

    gate_pre = jnp.dot(tok, wts[:, :512], preferred_element_type=f32)[:, :hidden]
    grad_hidden = jnp.dot(cot, wts[:, 384:], preferred_element_type=f32)[:, hidden - 384:]
    grad_up = (grad_hidden * jax.nn.silu(gate_pre)).astype(jnp.bfloat16)
    outer = jnp.dot(grad_up, proj_out, preferred_element_type=f32)
    inner = jnp.dot(tok, proj_in, preferred_element_type=f32)
    positions = jnp.arange(window, dtype=jnp.int32)
    live = (positions[None, :] >= (window - lengths)[:, None]).astype(f32) * loss_mask.astype(f32)
    weighted = inner.reshape(seq_count, window, -1) * live[:, :, None]
    feats = jnp.einsum("stk,stl->skl", weighted, outer.reshape(seq_count, window, -1), precision=HI)
    width = feats.shape[2]
    fp = feats.reshape(seq_count, cycles, cols, width).transpose(2, 1, 0, 3).reshape(cols, 16, 128)

    col_all, all3, d_own, d_other = exchange(fp, dp)

    fcol = col_all.reshape(rows, cycles, seq_count, width).transpose(0, 2, 1, 3).reshape(seqs, cycles * width)
    take = all3.reshape(cols, TAKE, 128)
    f0 = take[:, :64].reshape(cols, seqs, width).transpose(1, 0, 2).reshape(seqs, cols * width)
    frow = take[:, 64:].reshape(cols, 2, cycles, seq_count, width)
    frow = lax.dynamic_slice_in_dim(frow, lax.rem(r, 2) * band_rows, band_rows, 4)
    frow = frow.transpose(0, 1, 3, 2, 4).reshape(seqs, cycles * band_rows)

    u = factored(d_own, d_other, gp, f0, frow)

    update = lax.dot_general(frow, fcol, (((0,), (0,)), ((), ())), precision=HI, preferred_element_type=f32) / seqs
    updated = gram_in + update.reshape(cycles, band_rows, cycles, band_cols)
    strip = lax.dynamic_slice_in_dim(u, c * band_cols, band_cols, 0)
    tile = lax.dynamic_slice_in_dim(strip, r * band_rows, band_rows, 1)
    at_row = lax.broadcasted_iota(jnp.int32, tile.shape, 1) + r * band_rows
    at_col = lax.broadcasted_iota(jnp.int32, tile.shape, 0) + c * band_cols
    tile = jnp.where(at_row >= at_col, tile, 0.0)
    strip = jnp.concatenate([tile, strip[:, pw + band_rows:]], axis=1)
    panel = strip.T.reshape(cycles, band_rows, 1, band_cols)
    gram_next = jnp.concatenate([panel, updated[:, :, 1:]], axis=2)

    count = queries.shape[0]
    extra = u[:, pw:]
    solved = extra[:, :count]
    both = lax.dot_general(solved, extra, (((0,), (0,)), ((), ())), precision=HI, preferred_element_type=f32)
    scores = both[:, count:count + seq_count]
    tail = queries[:, 1:] - both[:, band_rows:].reshape(count, cycles - 1, band_rows)
    own = lax.dynamic_slice_in_dim(solved, r * band_rows, band_rows, 0).T
    query_next = jnp.concatenate([own[:, None], tail], axis=1)
    return gram_next, query_next, scores


def solution(mesh):
    return jax.shard_map(
        local,
        mesh=mesh,
        in_specs=(
            P("rows", "cols"), P("rows", "cols"), P("rows", "cols"), P("rows", "cols"), P(), P("cols", None),
            P("rows"), P("rows", None), P(None, "rows", None, "cols"), P("cols", None, "rows")),
        out_specs=(P(None, "rows", None, "cols"), P("cols", None, "rows"), P("cols", "rows")),
        check_vma=False,
    )
```

```python
import jax
import jax.numpy as jnp
from jax import lax
from jax.experimental import pallas as pl
from jax.experimental.pallas import tpu as pltpu
from jax.sharding import PartitionSpec as P

HI = lax.Precision.HIGHEST
NB = 128

NZ, NX, NY, NC = 8, 4, 8, 2
DIMS = (NZ, NX, NY, NC)
MESH = pl.DeviceIdType.MESH


def add(a, b):
    return tuple((p + q) % n for p, q, n in zip(a, b, DIMS))


def neg(a):
    return tuple((-p) % n for p, n in zip(a, DIMS))


class Msg:
    def __init__(self, array, part, origin, off, dep, size):
        self.array, self.part, self.origin, self.off, self.dep, self.size = array, part, origin, off, dep, size


def ring(msgs, array, part, axis, start, dep, size, plus, minus):
    arrivals = []
    for step, hops in ((1, plus), (-1, minus)):
        unit = tuple(step if a == axis else 0 for a in range(4))
        unit = tuple(u % n for u, n in zip(unit, DIMS))
        origin, last = start, dep
        for _ in range(hops):
            m = Msg(array, part, origin, unit, last, size)
            msgs.append(m)
            origin = add(origin, neg(unit))
            arrivals.append((origin, m))
            last = m
    return arrivals


def ordered(msgs):
    import heapq
    free, done, pending = {}, {}, []
    followers = {}
    for n, m in enumerate(msgs):
        if m.dep is None:
            heapq.heappush(pending, (0.0, n))
        else:
            followers.setdefault(id(m.dep), []).append(n)
    while pending:
        at, n = heapq.heappop(pending)
        m = msgs[n]
        near = m.off == (0, 0, 0, 1)
        rate, hop = (250e3, 0.9) if near else (45e3, 1.7)
        begin = max(at, free.get(m.off, 0.0))
        free[m.off] = begin + m.size / rate
        done[n] = free[m.off] + hop
        for f in followers.get(id(m), []):
            heapq.heappush(pending, (done[n], f))
    return done


def position():
    r, c = lax.axis_index("rows"), lax.axis_index("cols")
    return (r // NX, lax.rem(r, NX), c // NC, lax.rem(c, NC))


def moved(me, off):
    return tuple(p if o == 0 else lax.rem(p + o, n) for p, o, n in zip(me, off, DIMS))


def device(me, off):
    z, x, y, k = moved(me, off)
    return {"rows": z * NX + x, "cols": y * NC + k}


def greet(me, offs):
    both = sorted(set(offs) | set(neg(o) for o in offs))
    barrier = pltpu.get_barrier_semaphore()
    for o in both:
        pl.semaphore_signal(barrier, inc=1, device_id=device(me, o), device_id_type=MESH)
    pl.semaphore_wait(barrier, len(both))


SPLIT = 80


def gather_messages(tsize, gsize, wrow, depth):
    msgs = []
    here = (0, 0, 0, 0)
    core = (0, 0, 0, 1)
    held = []
    for array, size, plus, minus in (("tok", tsize, 4, 3), ("cot", tsize, 3, 4), ("gp", gsize, 4, 3)):
        held += [(array, size, here, None)]
        held += [(array, size, o, m) for o, m in ring(msgs, array, 0, 2, here, None, size, plus, minus)]
    for array, size, o, m in held:
        msgs.append(Msg(array, 0, o, core, m, size))
    size = wrow * SPLIT
    got = [(here, None)] + ring(msgs, "w", 0, 0, here, None, size, 4, 3)
    for o, m in got:
        even = o[0] % 2 == 0
        ring(msgs, "w", 0, 1, o, m, size, 2 if even else 1, 1 if even else 2)
    size = wrow * (depth - SPLIT)
    got = [(here, None)] + ring(msgs, "w", 1, 1, here, None, size, 2, 1)
    for o, m in got:
        even = o[1] % 2 == 0
        ring(msgs, "w", 1, 0, o, m, size, 4 if even else 3, 3 if even else 4)
    return msgs


def gather_kernel(msgs, order, tok, cot, w, gp, tok_all, cot_all, w_all, gp_all, send, recv, own):
    me = position()
    depth, width, band = w.shape[0], tok.shape[1], gp.shape[0]

    def place(array, part, origin):
        z, x, y, k = moved(me, origin)
        if array == "w":
            at, rows = (0, SPLIT) if part == 0 else (SPLIT, depth - SPLIT)
            return w_all.at[pl.ds(pl.multiple_of((z * NX + x) * depth + at, 16), rows), :]
        c = y * NC + k
        if array == "gp":
            return gp_all.at[pl.ds(pl.multiple_of(c * band, 8), band), :]
        whole = tok_all if array == "tok" else cot_all
        return whole.at[:, pl.ds(pl.multiple_of(c * width, 128), width)]

    def mine(array, part):
        if array == "w":
            at, rows = (0, SPLIT) if part == 0 else (SPLIT, depth - SPLIT)
            return w.at[pl.ds(at, rows), :]
        return {"tok": tok, "cot": cot, "gp": gp}[array]

    def copy(n):
        m = msgs[n]
        src = mine(m.array, m.part) if m.origin == (0, 0, 0, 0) else place(m.array, m.part, m.origin)
        return pltpu.make_async_remote_copy(
            src_ref=src, dst_ref=place(m.array, m.part, m.origin), send_sem=send.at[n], recv_sem=recv.at[n],
            device_id=device(me, m.off), device_id_type=MESH)

    def arrived(n):
        m = msgs[n]
        there = place(m.array, m.part, add(m.origin, neg(m.off)))
        pltpu.make_async_remote_copy(
            src_ref=there, dst_ref=there, send_sem=send.at[n], recv_sem=recv.at[n],
            device_id=device(me, m.off), device_id_type=MESH).wait_recv()

    here = (0, 0, 0, 0)
    kept = [pltpu.make_async_copy(mine(a, p), place(a, p, here), own.at[i])
            for i, (a, p) in enumerate((("tok", 0), ("cot", 0), ("gp", 0), ("w", 0), ("w", 1)))]
    for c in kept:
        c.start()
    greet(me, [m.off for m in msgs])
    for n, m in enumerate(msgs):
        if m.dep is None:
            copy(n).start()
    for n in order:
        arrived(n)
        for f, m in enumerate(msgs):
            if m.dep is msgs[n]:
                copy(f).start()
    for n in range(len(msgs)):
        copy(n).wait_send()
    for c in kept:
        c.wait()


def gather(tok, cot, w, gp):
    msgs = gather_messages(tok.size * 2, gp.size * 4, w.shape[1] * 2, w.shape[0])
    times = ordered(msgs)
    order = sorted(range(len(msgs)), key=lambda n: (times[n], n))
    vm = pl.BlockSpec(memory_space=pltpu.VMEM)

    def body(*refs):
        gather_kernel(msgs, order, *refs)
    rows = NZ * NX
    cols = NY * NC
    return pl.pallas_call(
        body,
        out_shape=(
            jax.ShapeDtypeStruct((tok.shape[0], tok.shape[1] * cols), tok.dtype),
            jax.ShapeDtypeStruct((cot.shape[0], cot.shape[1] * cols), cot.dtype),
            jax.ShapeDtypeStruct((w.shape[0] * rows, w.shape[1]), w.dtype),
            jax.ShapeDtypeStruct((gp.shape[0] * cols, gp.shape[1]), gp.dtype)),
        in_specs=[vm] * 4, out_specs=(vm,) * 4,
        scratch_shapes=[pltpu.SemaphoreType.DMA((len(msgs),)), pltpu.SemaphoreType.DMA((len(msgs),)),
                        pltpu.SemaphoreType.DMA((5,))],
        compiler_params=pltpu.CompilerParams(collective_id=0, has_side_effects=True, vmem_limit_bytes=4 << 20),
        name="gather",
    )(tok, cot, w, gp)


def exchange_messages(size):
    msgs = []
    here = (0, 0, 0, 0)
    held = []
    got = [(here, None)] + ring(msgs, "d", 0, 0, here, None, size, 4, 3)
    for o, m in got:
        even = o[0] % 2 == 0
        held += [(0, o, m)] + [(0, p, q) for p, q in ring(msgs, "d", 0, 1, o, m, size, 2 if even else 1, 1 if even else 2)]
    got = [(here, None)] + ring(msgs, "d", 1, 1, here, None, size, 2, 1)
    for o, m in got:
        even = o[1] % 2 == 0
        held += [(1, o, m)] + [(1, p, q) for p, q in ring(msgs, "d", 1, 0, o, m, size, 4 if even else 3, 3 if even else 4)]
    for part, o, m in held:
        msgs.append(Msg("d", part, o, (0, 0, 0, 1), m, size))
    return msgs


HALF = 512
TAKE = 96
SUM_AT, SPREAD_AT, PANEL_AT = 6.0, 10.0, 19.0


def exchange_kernel(msgs, times, fp, dp, col_all, all3, d_all, d_other,
                    parts, hbuf, p3, dsend, drecv, s1, r1, s2, r2, sl, rl, s3, r3, s4, r4, own):
    me = position()
    r, c = lax.axis_index("rows"), lax.axis_index("cols")
    here, core = (0, 0, 0, 0), (0, 0, 0, 1)
    band = dp.shape[0]
    half = band // 2

    def rdma(src, dst, send, recv, to):
        return pltpu.make_async_remote_copy(src_ref=src, dst_ref=dst, send_sem=send, recv_sem=recv,
                                            device_id=to, device_id_type=MESH)

    def row_of(origin, part):
        z, x, _, _ = moved(me, origin)
        return pl.ds(pl.multiple_of((z * NX + x) * band + half * part, 8), half)

    def dcopy(n):
        m = msgs[n]
        src = dp.at[pl.ds(half * m.part, half), :] if m.origin == here else d_all.at[row_of(m.origin, m.part), :]
        if m.off == core:
            src = (dp.at[pl.ds(half * m.part, half), pl.ds(0, HALF)] if m.origin == here
                   else d_all.at[row_of(m.origin, m.part), pl.ds(0, HALF)])
            dst = d_other.at[row_of(m.origin, m.part), :]
        else:
            dst = d_all.at[row_of(m.origin, m.part), :]
        return rdma(src, dst, dsend.at[n], drecv.at[n], device(me, m.off))

    def darrived(n):
        m = msgs[n]
        if m.off == core:
            there = d_other.at[row_of(m.origin, m.part), :]
        else:
            there = d_all.at[row_of(add(m.origin, neg(m.off)), m.part), :]
        rdma(there, there, dsend.at[n], drecv.at[n], device(me, m.off)).wait_recv()

    cols_off = [(0, 0, dy, dk) for dy in range(NY) for dk in range(NC) if (dy, dk) != (0, 0)]
    rows_off = [(dz, dx, 0, 0) for dz in range(NZ) for dx in range(NX) if (dz, dx) != (0, 0)]
    y_off = [(0, 0, dy, 0) for dy in range(1, NY)]
    legs = [{"rows": 2 * c + e, "cols": r // 2} for e in range(2)]
    at_home = [jnp.logical_and(c == r // 2, lax.rem(r, 2) == e) for e in range(2)]

    def col_of(off):
        _, _, y, k = moved(me, off)
        return y * NC + k

    kept = pltpu.make_async_copy(dp, d_all.at[pl.ds(pl.multiple_of(r * band, 8), band), :], own)
    kept.start()
    both = sorted(set(cols_off + rows_off))
    barrier = pltpu.get_barrier_semaphore()
    for o in both:
        pl.semaphore_signal(barrier, inc=1, device_id=device(me, o), device_id_type=MESH)
    for e in range(2):
        @pl.when(jnp.logical_not(at_home[e]))
        def _():
            pl.semaphore_signal(barrier, inc=1, device_id=legs[e], device_id_type=MESH)
    pl.semaphore_wait(barrier, jnp.where(c == r // 2, len(both) + 1, len(both) + 2))

    first = [rdma(fp.at[col_of(o)], parts.at[i], s1.at[i], r1.at[i], device(me, o)) for i, o in enumerate(cols_off)]
    my_rows = pl.ds(pl.multiple_of(r * 16, 16), 16)
    second = [rdma(hbuf, col_all.at[my_rows, :], s2.at[i], r2.at[i], device(me, o)) for i, o in enumerate(rows_off)]
    leg_to = p3.at[pl.ds(pl.multiple_of(64 + lax.rem(r, 2) * 16, 16), 16), :]
    leg = [rdma(hbuf, leg_to, sl.at[e], rl.at[lax.rem(r, 2)], legs[e]) for e in range(2)]
    my_take = pl.ds(pl.multiple_of(c * TAKE, 8), TAKE)
    third = [rdma(p3, all3.at[my_take, :], s3.at[i], r3.at[i], device(me, o)) for i, o in enumerate(y_off)]

    def take_of(off):
        return all3.at[pl.ds(pl.multiple_of(col_of(off) * TAKE, 8), TAKE), :]

    def give(i):
        off = here if i == 0 else neg(y_off[i - 1])
        src = p3 if i == 0 else take_of(off)
        return rdma(src, take_of(off), s4.at[i], r4.at[i], device(me, core))

    def sum_up():
        total = fp[c]
        for i in range(len(cols_off)):
            first[i].wait_recv()
            total = total + parts[i]
        hbuf[...] = total
        col_all[my_rows, :] = total
        for e in range(2):
            @pl.when(jnp.logical_not(at_home[e]))
            def _():
                leg[e].start()

            @pl.when(at_home[e])
            def _():
                p3[pl.ds(64 + 16 * e, 16), :] = total
        for copy in second:
            copy.start()

    def spread():
        for i, o in enumerate(rows_off):
            z, x, _, _ = moved(me, neg(o))
            there = col_all.at[pl.ds(pl.multiple_of((z * NX + x) * 16, 16), 16), :]
            rdma(there, there, s2.at[i], r2.at[i], device(me, o)).wait_recv()
        for n in range(2 * NZ * NX):
            p3[pl.ds(n, 1), :] = col_all[pl.ds(8 * n, 1), :]
        for e in range(2):
            @pl.when(jnp.logical_not(at_home[e]))
            def _():
                there = p3.at[pl.ds(64 + 16 * e, 16), :]
                rdma(there, there, sl.at[e], rl.at[e], legs[e]).wait_recv()
        all3[my_take, :] = p3[...]
        for copy in third:
            copy.start()
        give(0).start()

    def panel():
        for i, o in enumerate(y_off):
            there = take_of(neg(o))
            rdma(there, there, s3.at[i], r3.at[i], device(me, o)).wait_recv()
            give(i + 1).start()

    for copy in first:
        copy.start()
    for n, m in enumerate(msgs):
        if m.dep is None:
            dcopy(n).start()
    events = sorted([(times[n], n) for n in range(len(msgs))]
                    + [(SUM_AT, -1), (SPREAD_AT, -2), (PANEL_AT, -3)])
    for _, n in events:
        if n < 0:
            (sum_up, spread, panel)[-n - 1]()
            continue
        darrived(n)
        for f, m in enumerate(msgs):
            if m.dep is msgs[n]:
                dcopy(f).start()
    for i in range(NY):
        off = here if i == 0 else neg(y_off[i - 1])
        there = take_of(add(off, core))
        rdma(there, there, s4.at[i], r4.at[i], device(me, core)).wait_recv()
    for n in range(len(msgs)):
        dcopy(n).wait_send()
    for copy in first + second + third:
        copy.wait_send()
    for e in range(2):
        @pl.when(jnp.logical_not(at_home[e]))
        def _():
            leg[e].wait_send()
    for i in range(NY):
        give(i).wait_send()
    kept.wait()


def exchange(fp, dp):
    msgs = exchange_messages(dp.size * 2)
    times = ordered(msgs)
    vm = pl.BlockSpec(memory_space=pltpu.VMEM)
    f32 = jnp.float32
    rows, cols = NZ * NX, NY * NC
    dma = pltpu.SemaphoreType.DMA

    def body(*refs):
        exchange_kernel(msgs, times, *refs)
    return pl.pallas_call(
        body,
        out_shape=(
            jax.ShapeDtypeStruct((rows * 16, 128), f32),
            jax.ShapeDtypeStruct((cols * TAKE, 128), f32),
            jax.ShapeDtypeStruct((rows * dp.shape[0], dp.shape[1]), f32),
            jax.ShapeDtypeStruct((rows * dp.shape[0], HALF), f32)),
        in_specs=[vm] * 2, out_specs=(vm,) * 4,
        scratch_shapes=[
            pltpu.VMEM((cols - 1, 16, 128), f32), pltpu.VMEM((16, 128), f32), pltpu.VMEM((TAKE, 128), f32),
            dma((len(msgs),)), dma((len(msgs),)), dma((cols - 1,)), dma((cols - 1,)), dma((rows - 1,)), dma((rows - 1,)),
            dma((2,)), dma((2,)), dma((NY - 1,)), dma((NY - 1,)), dma((NY,)), dma((NY,)), dma],
        compiler_params=pltpu.CompilerParams(collective_id=1, has_side_effects=True, vmem_limit_bytes=4 << 20),
        name="exchange",
    )(fp, dp)


def lanes(x, j):
    return jnp.broadcast_to(x[:, j:j + 1], x.shape)


def subl(x, k):
    return jnp.broadcast_to(x[k:k + 1, :], x.shape)


def factor_block(A, V, group=8):
    n = len(A)
    A, V = list(A), list(V)
    sub = lax.broadcasted_iota(jnp.int32, (8, NB), 0)
    for g in range(0, n, group):
        for p in range(g, g + group):
            a, v = A[p], V[p]
            C = [lanes(a, 8 * p + j) for j in range(8)]
            Us, Vs, R, S = [], [], [], []
            for k in range(8):
                r = lax.rsqrt(subl(C[k], k))
                sb = [subl(C[k], j) if j > k else None for j in range(8)]
                Cs = C[k] * (r * r)
                for j in range(k + 1, 8):
                    C[j] = C[j] - Cs * sb[j]
                R.append(r)
                S.append([None if t is None else t * r for t in sb])
                uk, vk = subl(a, k) * r, subl(v, k) * r
                m = jnp.where(sub > k, C[k] * r, 0.0)
                a, v = a - m * uk, v - m * vk
                Us.append(uk)
                Vs.append(vk)
            un, vn = Us[0], Vs[0]
            for k in range(1, 8):
                un = jnp.where(sub == k, Us[k], un)
                vn = jnp.where(sub == k, Vs[k], vn)
            A[p], V[p] = un, vn
            for q in range(p + 1, g + group):
                aq, vq = A[q], V[q]
                G = [lanes(aq, 8 * p + j) for j in range(8)]
                L = []
                for k in range(8):
                    t = G[k]
                    for m in range(k):
                        t = t - L[m] * S[m][k]
                    L.append(t * R[k])
                for k in range(8):
                    aq, vq = aq - L[k] * Us[k], vq - L[k] * Vs[k]
                A[q], V[q] = aq, vq
        if g + group < n:
            ug = jnp.concatenate(A[g:g + group], 0)
            vg = jnp.concatenate(V[g:g + group], 0)
            change = tdot(ug, jnp.concatenate([ug, vg], 1), HI)
            for q in range(g + group, n):
                A[q] = A[q] - change[8 * q:8 * q + 8, :NB]
                V[q] = V[q] - change[8 * q:8 * q + 8, NB:]
    return A, V


def split3(x):
    h = x.astype(jnp.bfloat16)
    rest = x - h.astype(jnp.float32)
    m = rest.astype(jnp.bfloat16)
    return h, m, (rest - m.astype(jnp.float32)).astype(jnp.bfloat16)


def tdot(a, b, precision=None):
    return lax.dot_general(a, b, (((0,), (0,)), ((), ())), precision=precision, preferred_element_type=jnp.float32)


def paired(even, odd, lane):
    return jnp.where(lane < 64, even, pltpu.roll(odd, 64, 1)), jnp.where(lane < 64, pltpu.roll(even, 64, 1), odd)


def factor_kernel(x, y, gp, all3, col_all, upd, both, strip, own, u, inv, hh, hm, ml, mh, rowp, frow, fcol):
    n, width = u.shape
    nb, half = n // NB, n // 2
    r, c = lax.axis_index("rows"), lax.axis_index("cols")
    k = lax.rem(c, NC)
    cols = NY * NC
    seqs = 128
    per = seqs // (NZ * NX)
    heads = 16
    lane64 = lax.broadcasted_iota(jnp.int32, (64, NB), 1)

    def keep(h, m, l, cs):
        hh[pl.ds(0, NB), cs] = h
        hh[pl.ds(NB, NB), cs] = h
        hm[pl.ds(0, NB), cs] = h
        hm[pl.ds(NB, NB), cs] = m
        ml[pl.ds(0, NB), cs] = m
        ml[pl.ds(NB, NB), cs] = l
        mh[pl.ds(0, NB), cs] = m
        mh[pl.ds(NB, NB), cs] = h

    def product(qs, cs):
        return tdot(hh[:, qs], hm[:, cs]) + (tdot(ml[:, qs], hh[:, cs]) + tdot(mh[:, qs], ml[:, cs]))

    for p in range(cols // 2):
        top, low = paired(all3[pl.ds(2 * p * TAKE, 64), :], all3[pl.ds((2 * p + 1) * TAKE, 64), :], lane64)
        keep(*split3(jnp.concatenate([top, low], 0)), pl.ds(p * NB, NB))
    for p in range(cols):
        rowp[pl.ds(32 * p, 32), :] = all3[pl.ds(p * TAKE + 64, 32), :]
    for p in range(4):
        top, low = paired(col_all[pl.ds(2 * p, 64, stride=8), :], col_all[pl.ds(2 * p + 1, 64, stride=8), :], lane64)
        fcol[pl.ds(0, 64), pl.ds(p * NB, NB)] = top
        fcol[pl.ds(64, 64), pl.ds(p * NB, NB)] = low
    second = lax.rem(r, 2) == 1
    for t in range(2):
        top = low = jnp.zeros((64, NB), jnp.float32)
        for q in range(4):
            piece = rowp[pl.ds(4 * t + q, 64, stride=8), :]
            piece = jnp.where(second, pltpu.roll(piece, 96, 1), piece)
            here = lane64 // 32 == q
            top = jnp.where(here, piece if q == 0 else pltpu.roll(piece, 32 * q, 1), top)
            low = jnp.where(here, piece if q == 2 else pltpu.roll(piece, (32 * q + 64) % 128, 1), low)
        frow[pl.ds(0, 64), pl.ds(t * NB, NB)] = top
        frow[pl.ds(64, 64), pl.ds(t * NB, NB)] = low
    at = lax.broadcasted_iota(jnp.int32, (seqs, NB), 0)
    lane = lax.broadcasted_iota(jnp.int32, (seqs, NB), 1)
    seq = 2 * (at - jnp.where(at >= 64, 64, 0)) + jnp.where(at >= 64, 1, 0)
    wanted = jnp.logical_and(jnp.logical_and(lane >= heads, lane < heads + per), seq == per * r + lane - heads)
    pick = jnp.where(wanted, jnp.float32(seqs), 0.0)
    keep(*split3(jnp.where(lane < 32, pick, frow[:, :NB])), pl.ds(n, NB))
    keep(*split3(frow[:, NB:]), pl.ds(n + NB, NB))
    upd[...] = tdot(frow[...], fcol[...], HI) * (1.0 / seqs)

    for b in range(nb):
        rows = pl.ds(b * NB, NB)
        u[rows, pl.ds(pl.multiple_of(k * HALF, HALF), HALF)] = x[rows, :HALF]
        u[rows, pl.ds(pl.multiple_of((1 - k) * HALF, HALF), HALF)] = y[rows, :]
        u[rows, n:n + NB] = jnp.where(lane < heads, x[rows, HALF:], jnp.where(lane < 32, 0.0, gp[rows, :NB]))
        u[rows, n + NB:] = gp[rows, NB:]
        cs = pl.ds(b * NB, width - b * NB)
        u[rows, cs] = u[rows, cs] + product(rows, cs) * (1.0 / seqs)

    row = lax.broadcasted_iota(jnp.int32, (8, NB), 0)
    col = lax.broadcasted_iota(jnp.int32, (8, NB), 1)

    def outer(b, _):
        o = pl.multiple_of(b * NB, NB)
        rows = pl.ds(o, NB)
        A = [u[pl.ds(o + 8 * p, 8), rows] for p in range(NB // 8)]
        V = [jnp.where(col == row + 8 * p, 1.0, 0.0) for p in range(NB // 8)]
        A, V = factor_block(A, V)
        for p in range(NB // 8):
            inv[pl.ds(8 * p, 8), :] = V[p]
        ih, im, il = split3(inv[...])
        hh_l, ml_l, mh_l = (jnp.concatenate(pair, 1) for pair in ((ih, ih), (im, il), (im, ih)))

        def dot(a, top, low):
            return jnp.dot(a, jnp.concatenate([top, low], 0), preferred_element_type=jnp.float32)

        def scale(lo, hi):
            for t in range(lo, hi, 256):
                cs = pl.ds(t, 256)
                h, m, l = split3(u[rows, cs])
                new = dot(hh_l, h, m) + (dot(ml_l, h, h) + dot(mh_l, m, l))
                u[rows, cs] = new
                keep(*split3(new), cs)

        @pl.when(b < nb // 2)
        def _():
            scale(0, half)
        scale(half, width)
        for p in range(NB // 8):
            u[pl.ds(o + 8 * p, 8), rows] = jnp.where(col >= row + 8 * p, A[p], 0.0)

        def trail(lo):
            def body(q, _):
                qs = pl.ds(pl.multiple_of(q * NB, NB), NB)
                cs = pl.ds(lo, width - lo)
                u[qs, cs] = u[qs, cs] - product(qs, cs)
                return 0
            return body
        lax.fori_loop(b + 1, nb // 2, trail(0), 0)
        lax.fori_loop(jnp.maximum(b + 1, nb // 2), nb, trail(half), 0)
        return 0
    lax.fori_loop(0, nb, outer, 0)

    extra = pl.ds(n, width - n)
    both[...] = tdot(u[:, n:n + NB], u[:, n:], HI)[:heads]
    own[...] = u[pl.ds(pl.multiple_of(32 * r, 32), 32), n:n + NB]
    mine = pl.ds(pl.multiple_of(64 * c, 64), 64)
    tile = pltpu.roll(u[mine, pl.ds(pl.multiple_of((r // 4) * NB, NB), NB)], lax.rem(128 - 32 * lax.rem(r, 4), 128), 1)
    down = lax.broadcasted_iota(jnp.int32, (64, NB), 0) + 64 * c
    tile = jnp.where(lane64 + 32 * r >= down, tile, 0.0)
    strip[:, :NB] = jnp.where(lane64 < 32, tile, u[mine, n:n + NB])
    strip[:, NB:] = u[mine, n + NB:]


def factored(x, y, gp, all3, col_all):
    n, f32 = x.shape[0], jnp.float32
    vm = pl.BlockSpec(memory_space=pltpu.VMEM)
    packed = pltpu.VMEM((2 * NB, n + 256), jnp.bfloat16)
    return pl.pallas_call(
        factor_kernel,
        out_shape=(
            jax.ShapeDtypeStruct((256, 512), f32), jax.ShapeDtypeStruct((16, 256), f32),
            jax.ShapeDtypeStruct((64, 256), f32), jax.ShapeDtypeStruct((32, 128), f32)),
        in_specs=[vm] * 5, out_specs=(vm,) * 4,
        scratch_shapes=[
            pltpu.VMEM((n, n + 256), f32), pltpu.VMEM((NB, NB), f32), packed, packed, packed, packed,
            pltpu.VMEM((512, NB), f32), pltpu.VMEM((NB, 256), f32), pltpu.VMEM((NB, 512), f32)],
        compiler_params=pltpu.CompilerParams(vmem_limit_bytes=20 << 20),
        name="factor",
    )(x, y, gp, all3, col_all)


def features_kernel(tok, cot, wts, proj_in, proj_out, live, fp, block):
    f32 = jnp.float32
    hidden = 448
    depth, step = tok.shape[1], 512

    def body(i, acc):
        at = pl.multiple_of(i * step, step)
        cs, t = pl.ds(at, step), tok[:, pl.ds(at, step)]
        g, h, p = acc
        return (g + jnp.dot(t, wts[cs, :512], preferred_element_type=f32),
                h + jnp.dot(cot[:, cs], wts[cs, 384:], preferred_element_type=f32),
                p + jnp.dot(t, proj_in[cs, :], preferred_element_type=f32))
    rows = tok.shape[0]
    g, h, p = lax.fori_loop(0, depth // step, body, (
        jnp.zeros((rows, 512), f32), jnp.zeros((rows, 512), f32), jnp.zeros((rows, 128), f32)))
    h = pltpu.roll(h, 512 - 64, 1)
    lane = lax.broadcasted_iota(jnp.int32, (rows, 512), 1)
    up = jnp.where(lane < hidden, h * (g / (1.0 + jnp.exp(-g))), 0.0).astype(jnp.bfloat16)
    outer = jnp.dot(up, proj_out[...], preferred_element_type=f32)
    p = p * live[...]
    for s in range(2):
        total = jnp.zeros((128, 128), f32)
        for e in range(2):
            ts = slice((2 * s + e) * 64, (2 * s + e + 1) * 64)
            o = outer[ts] if e == 0 else pltpu.roll(outer[ts], 64, 1)
            total = total + tdot(p[ts], o, HI)
        block[...] = total
        for c in range(16):
            fp[c, pl.ds(8 * s, 8), :] = block[pl.ds(c, 8, stride=16), :]


def local(tokens, cotangent, gate_weight, down_weight, proj_in, proj_out, lengths, loss_mask, gram_in, queries):
    f32 = jnp.float32
    r, c = lax.axis_index("rows"), lax.axis_index("cols")
    k = lax.rem(c, NC)
    cycles, band_rows, _, band_cols = gram_in.shape
    seq_count, window = loss_mask.shape
    vm = pl.BlockSpec(memory_space=pltpu.VMEM)

    weights = jnp.concatenate([gate_weight, down_weight], axis=1)
    band = gram_in[:, :, 0, :].reshape(cycles * band_rows, band_cols).T
    positions = jnp.arange(window, dtype=jnp.int32)
    live = (positions[None, :] >= (window - lengths)[:, None]).astype(f32) * loss_mask.astype(f32)
    outer_in = jnp.pad(proj_out, ((0, 512 - proj_out.shape[0]), (0, 128 - proj_out.shape[1])))
    live = jnp.broadcast_to(live.reshape(seq_count * window, 1), (seq_count * window, proj_in.shape[1]))
    weights, band, outer_in, live = lax.optimization_barrier((weights, band, outer_in, live))
    tok, cot, wts, gp = gather(tokens, cotangent, weights, band)

    fp = pl.pallas_call(
        features_kernel,
        out_shape=jax.ShapeDtypeStruct((NY * NC, 16, 128), f32),
        in_specs=[vm] * 6, out_specs=vm,
        scratch_shapes=[pltpu.VMEM((128, 128), f32)],
        compiler_params=pltpu.CompilerParams(vmem_limit_bytes=12 << 20),
        name="features",
    )(tok, cot, wts, proj_in, outer_in, live)

    gp, fp = lax.optimization_barrier((gp, fp))
    diag = gp[:, :band_rows].T
    diag = lax.dynamic_slice_in_dim(diag, k * HALF, HALF, 1)
    head = jnp.pad(queries[:, 0, :].T, ((0, 0), (0, 128 - queries.shape[0])))
    dp = jnp.concatenate([diag, head], axis=1)

    col_all, all3, d_own, d_other = exchange(fp, dp)
    upd, both, strip, own = factored(d_own, d_other, gp, all3, col_all)

    panel = strip.T.reshape(cycles, band_rows, 1, band_cols)
    which = lax.broadcasted_iota(jnp.int32, gram_in.shape, 2)
    gram_next = jnp.where(which == 0, panel, gram_in + upd.reshape(gram_in.shape))
    count = queries.shape[0]
    scores = both[:, count:count + seq_count]
    tail = queries[:, 1:] - both[:, band_rows:].reshape(count, cycles - 1, band_rows)
    query_next = jnp.concatenate([own[:, :count].T[:, None], tail], axis=1)
    return gram_next, query_next, scores


def solution(mesh):
    return jax.shard_map(
        local,
        mesh=mesh,
        in_specs=(
            P("rows", "cols"), P("rows", "cols"), P("rows", "cols"), P("rows", "cols"), P(), P("cols", None),
            P("rows"), P("rows", None), P(None, "rows", None, "cols"), P("cols", None, "rows")),
        out_specs=(P(None, "rows", None, "cols"), P("cols", None, "rows"), P("cols", "rows")),
        check_vma=False,
    )
```

```python
import jax
import jax.numpy as jnp
from jax import lax
from jax.experimental import pallas as pl
from jax.experimental.pallas import tpu as pltpu
from jax.sharding import PartitionSpec as P

HI = lax.Precision.HIGHEST
NB = 128

NZ, NX, NY, NC = 8, 4, 8, 2
DIMS = (NZ, NX, NY, NC)
MESH = pl.DeviceIdType.MESH


def add(a, b):
    return tuple((p + q) % n for p, q, n in zip(a, b, DIMS))


def neg(a):
    return tuple((-p) % n for p, n in zip(a, DIMS))


class Msg:
    def __init__(self, array, part, origin, off, dep, size):
        self.array, self.part, self.origin, self.off, self.dep, self.size = array, part, origin, off, dep, size


def ring(msgs, array, part, axis, start, dep, size, plus, minus):
    arrivals = []
    for step, hops in ((1, plus), (-1, minus)):
        unit = tuple(step if a == axis else 0 for a in range(4))
        unit = tuple(u % n for u, n in zip(unit, DIMS))
        origin, last = start, dep
        for _ in range(hops):
            m = Msg(array, part, origin, unit, last, size)
            msgs.append(m)
            origin = add(origin, neg(unit))
            arrivals.append((origin, m))
            last = m
    return arrivals


def ordered(msgs):
    import heapq
    free, done, pending = {}, {}, []
    followers = {}
    for n, m in enumerate(msgs):
        if m.dep is None:
            heapq.heappush(pending, (0.0, n))
        else:
            followers.setdefault(id(m.dep), []).append(n)
    while pending:
        at, n = heapq.heappop(pending)
        m = msgs[n]
        near = m.off == (0, 0, 0, 1)
        rate, hop = (250e3, 0.9) if near else (45e3, 1.7)
        begin = max(at, free.get(m.off, 0.0))
        free[m.off] = begin + m.size / rate
        done[n] = free[m.off] + hop
        for f in followers.get(id(m), []):
            heapq.heappush(pending, (done[n], f))
    return done


def position():
    r, c = lax.axis_index("rows"), lax.axis_index("cols")
    return (r // NX, lax.rem(r, NX), c // NC, lax.rem(c, NC))


def moved(me, off):
    return tuple(p if o == 0 else lax.rem(p + o, n) for p, o, n in zip(me, off, DIMS))


def device(me, off):
    z, x, y, k = moved(me, off)
    return {"rows": z * NX + x, "cols": y * NC + k}


def greet(me, offs):
    both = sorted(set(offs) | set(neg(o) for o in offs))
    barrier = pltpu.get_barrier_semaphore()
    for o in both:
        pl.semaphore_signal(barrier, inc=1, device_id=device(me, o), device_id_type=MESH)
    pl.semaphore_wait(barrier, len(both))


SPLIT = 80


def gather_messages(tsize, gsize, wrow, depth):
    msgs = []
    here = (0, 0, 0, 0)
    core = (0, 0, 0, 1)
    held = []
    for array, size, plus, minus in (("tok", tsize, 4, 3), ("cot", tsize, 3, 4), ("gp", gsize, 4, 3)):
        held += [(array, size, here, None)]
        held += [(array, size, o, m) for o, m in ring(msgs, array, 0, 2, here, None, size, plus, minus)]
    for array, size, o, m in held:
        msgs.append(Msg(array, 0, o, core, m, size))
    size = wrow * SPLIT
    got = [(here, None)] + ring(msgs, "w", 0, 0, here, None, size, 4, 3)
    for o, m in got:
        even = o[0] % 2 == 0
        ring(msgs, "w", 0, 1, o, m, size, 2 if even else 1, 1 if even else 2)
    size = wrow * (depth - SPLIT)
    got = [(here, None)] + ring(msgs, "w", 1, 1, here, None, size, 2, 1)
    for o, m in got:
        even = o[1] % 2 == 0
        ring(msgs, "w", 1, 0, o, m, size, 4 if even else 3, 3 if even else 4)
    return msgs


def gather_kernel(msgs, order, tok, cot, w, gp, tok_all, cot_all, w_all, gp_all, send, recv, own):
    me = position()
    depth, width, band = w.shape[0], tok.shape[1], gp.shape[0]

    def place(array, part, origin):
        z, x, y, k = moved(me, origin)
        if array == "w":
            at, rows = (0, SPLIT) if part == 0 else (SPLIT, depth - SPLIT)
            return w_all.at[pl.ds(pl.multiple_of((z * NX + x) * depth + at, 16), rows), :]
        c = y * NC + k
        if array == "gp":
            return gp_all.at[pl.ds(pl.multiple_of(c * band, 8), band), :]
        whole = tok_all if array == "tok" else cot_all
        return whole.at[:, pl.ds(pl.multiple_of(c * width, 128), width)]

    def mine(array, part):
        if array == "w":
            at, rows = (0, SPLIT) if part == 0 else (SPLIT, depth - SPLIT)
            return w.at[pl.ds(at, rows), :]
        return {"tok": tok, "cot": cot, "gp": gp}[array]

    def copy(n):
        m = msgs[n]
        src = mine(m.array, m.part) if m.origin == (0, 0, 0, 0) else place(m.array, m.part, m.origin)
        return pltpu.make_async_remote_copy(
            src_ref=src, dst_ref=place(m.array, m.part, m.origin), send_sem=send.at[n], recv_sem=recv.at[n],
            device_id=device(me, m.off), device_id_type=MESH)

    def arrived(n):
        m = msgs[n]
        there = place(m.array, m.part, add(m.origin, neg(m.off)))
        pltpu.make_async_remote_copy(
            src_ref=there, dst_ref=there, send_sem=send.at[n], recv_sem=recv.at[n],
            device_id=device(me, m.off), device_id_type=MESH).wait_recv()

    here = (0, 0, 0, 0)
    kept = [pltpu.make_async_copy(mine(a, p), place(a, p, here), own.at[i])
            for i, (a, p) in enumerate((("tok", 0), ("cot", 0), ("gp", 0), ("w", 0), ("w", 1)))]
    for c in kept:
        c.start()
    greet(me, [m.off for m in msgs])
    for n, m in enumerate(msgs):
        if m.dep is None:
            copy(n).start()
    for n in order:
        arrived(n)
        for f, m in enumerate(msgs):
            if m.dep is msgs[n]:
                copy(f).start()
    for n in range(len(msgs)):
        copy(n).wait_send()
    for c in kept:
        c.wait()


def gather(tok, cot, w, gp):
    msgs = gather_messages(tok.size * 2, gp.size * 4, w.shape[1] * 2, w.shape[0])
    times = ordered(msgs)
    order = sorted(range(len(msgs)), key=lambda n: (times[n], n))
    vm = pl.BlockSpec(memory_space=pltpu.VMEM)

    def body(*refs):
        gather_kernel(msgs, order, *refs)
    rows = NZ * NX
    cols = NY * NC
    return pl.pallas_call(
        body,
        out_shape=(
            jax.ShapeDtypeStruct((tok.shape[0], tok.shape[1] * cols), tok.dtype),
            jax.ShapeDtypeStruct((cot.shape[0], cot.shape[1] * cols), cot.dtype),
            jax.ShapeDtypeStruct((w.shape[0] * rows, w.shape[1]), w.dtype),
            jax.ShapeDtypeStruct((gp.shape[0] * cols, gp.shape[1]), gp.dtype)),
        in_specs=[vm] * 4, out_specs=(vm,) * 4,
        scratch_shapes=[pltpu.SemaphoreType.DMA((len(msgs),)), pltpu.SemaphoreType.DMA((len(msgs),)),
                        pltpu.SemaphoreType.DMA((5,))],
        compiler_params=pltpu.CompilerParams(collective_id=0, has_side_effects=True, vmem_limit_bytes=4 << 20),
        name="gather",
    )(tok, cot, w, gp)


def exchange_messages(size):
    msgs = []
    here = (0, 0, 0, 0)
    held = []
    got = [(here, None)] + ring(msgs, "d", 0, 0, here, None, size, 4, 3)
    for o, m in got:
        even = o[0] % 2 == 0
        held += [(0, o, m)] + [(0, p, q) for p, q in ring(msgs, "d", 0, 1, o, m, size, 2 if even else 1, 1 if even else 2)]
    got = [(here, None)] + ring(msgs, "d", 1, 1, here, None, size, 2, 1)
    for o, m in got:
        even = o[1] % 2 == 0
        held += [(1, o, m)] + [(1, p, q) for p, q in ring(msgs, "d", 1, 0, o, m, size, 4 if even else 3, 3 if even else 4)]
    for part, o, m in held:
        msgs.append(Msg("d", part, o, (0, 0, 0, 1), m, size))
    return msgs


HALF = 512
TAKE = 96
BEGIN_AT, SUM_AT, SPREAD_AT, PANEL_AT = 3.2, 9.0, 13.0, 21.0


def exchange_kernel(msgs, times, tok, cot, wts, proj_in, proj_out, live, gp, head, col_all, all3, d_all, d_other,
                    fp, dp, block, parts, hbuf, p3, dsend, drecv, s1, r1, s2, r2, sl, rl, s3, r3, s4, r4, own):
    me = position()
    r, c = lax.axis_index("rows"), lax.axis_index("cols")
    here, core = (0, 0, 0, 0), (0, 0, 0, 1)
    band = head.shape[0]
    half = band // 2

    def rdma(src, dst, send, recv, to):
        return pltpu.make_async_remote_copy(src_ref=src, dst_ref=dst, send_sem=send, recv_sem=recv,
                                            device_id=to, device_id_type=MESH)

    def row_of(origin, part):
        z, x, _, _ = moved(me, origin)
        return pl.ds(pl.multiple_of((z * NX + x) * band + half * part, 8), half)

    def dcopy(n):
        m = msgs[n]
        src = dp.at[pl.ds(half * m.part, half), :] if m.origin == here else d_all.at[row_of(m.origin, m.part), :]
        if m.off == core:
            src = (dp.at[pl.ds(half * m.part, half), pl.ds(0, HALF)] if m.origin == here
                   else d_all.at[row_of(m.origin, m.part), pl.ds(0, HALF)])
            dst = d_other.at[row_of(m.origin, m.part), :]
        else:
            dst = d_all.at[row_of(m.origin, m.part), :]
        return rdma(src, dst, dsend.at[n], drecv.at[n], device(me, m.off))

    def darrived(n):
        m = msgs[n]
        if m.off == core:
            there = d_other.at[row_of(m.origin, m.part), :]
        else:
            there = d_all.at[row_of(add(m.origin, neg(m.off)), m.part), :]
        rdma(there, there, dsend.at[n], drecv.at[n], device(me, m.off)).wait_recv()

    cols_off = [(0, 0, dy, dk) for dy in range(NY) for dk in range(NC) if (dy, dk) != (0, 0)]
    rows_off = [(dz, dx, 0, 0) for dz in range(NZ) for dx in range(NX) if (dz, dx) != (0, 0)]
    y_off = [(0, 0, dy, 0) for dy in range(1, NY)]
    legs = [{"rows": 2 * c + e, "cols": r // 2} for e in range(2)]
    at_home = [jnp.logical_and(c == r // 2, lax.rem(r, 2) == e) for e in range(2)]

    def col_of(off):
        _, _, y, k = moved(me, off)
        return y * NC + k

    kept = pltpu.make_async_copy(dp, d_all.at[pl.ds(pl.multiple_of(r * band, 8), band), :], own)
    both = sorted(set(cols_off + rows_off))
    barrier = pltpu.get_barrier_semaphore()
    for o in both:
        pl.semaphore_signal(barrier, inc=1, device_id=device(me, o), device_id_type=MESH)
    for e in range(2):
        @pl.when(jnp.logical_not(at_home[e]))
        def _():
            pl.semaphore_signal(barrier, inc=1, device_id=legs[e], device_id_type=MESH)
    first = [rdma(fp.at[col_of(o)], parts.at[i], s1.at[i], r1.at[i], device(me, o)) for i, o in enumerate(cols_off)]
    my_rows = pl.ds(pl.multiple_of(r * 16, 16), 16)
    second = [rdma(hbuf, col_all.at[my_rows, :], s2.at[i], r2.at[i], device(me, o)) for i, o in enumerate(rows_off)]
    leg_to = p3.at[pl.ds(pl.multiple_of(64 + lax.rem(r, 2) * 16, 16), 16), :]
    leg = [rdma(hbuf, leg_to, sl.at[e], rl.at[lax.rem(r, 2)], legs[e]) for e in range(2)]
    my_take = pl.ds(pl.multiple_of(c * TAKE, 8), TAKE)
    third = [rdma(p3, all3.at[my_take, :], s3.at[i], r3.at[i], device(me, o)) for i, o in enumerate(y_off)]

    def take_of(off):
        return all3.at[pl.ds(pl.multiple_of(col_of(off) * TAKE, 8), TAKE), :]

    def give(i):
        off = here if i == 0 else neg(y_off[i - 1])
        src = p3 if i == 0 else take_of(off)
        return rdma(src, take_of(off), s4.at[i], r4.at[i], device(me, core))

    def sum_up():
        total = fp[c]
        for i in range(len(cols_off)):
            first[i].wait_recv()
            total = total + parts[i]
        hbuf[...] = total
        col_all[my_rows, :] = total
        for e in range(2):
            @pl.when(jnp.logical_not(at_home[e]))
            def _():
                leg[e].start()

            @pl.when(at_home[e])
            def _():
                p3[pl.ds(64 + 16 * e, 16), :] = total
        for copy in second:
            copy.start()

    def spread():
        for i, o in enumerate(rows_off):
            z, x, _, _ = moved(me, neg(o))
            there = col_all.at[pl.ds(pl.multiple_of((z * NX + x) * 16, 16), 16), :]
            rdma(there, there, s2.at[i], r2.at[i], device(me, o)).wait_recv()
        for n in range(2 * NZ * NX):
            p3[pl.ds(n, 1), :] = col_all[pl.ds(8 * n, 1), :]
        for e in range(2):
            @pl.when(jnp.logical_not(at_home[e]))
            def _():
                there = p3.at[pl.ds(64 + 16 * e, 16), :]
                rdma(there, there, sl.at[e], rl.at[e], legs[e]).wait_recv()
        all3[my_take, :] = p3[...]
        for copy in third:
            copy.start()
        give(0).start()

    def panel():
        for i, o in enumerate(y_off):
            there = take_of(neg(o))
            rdma(there, there, s3.at[i], r3.at[i], device(me, o)).wait_recv()
            give(i + 1).start()

    mine = gp[pl.ds(pl.multiple_of(lax.rem(c, NC) * HALF, HALF), HALF), :128]
    dp[:, :HALF] = mine.T[:band]
    dp[:, HALF:] = head[...]
    sums = features_part(tok, cot, wts, proj_in, 0, 5, None)
    pl.semaphore_wait(barrier, jnp.where(c == r // 2, len(both) + 1, len(both) + 2))
    kept.start()
    for n, m in enumerate(msgs):
        if m.dep is None:
            dcopy(n).start()
    sums = features_part(tok, cot, wts, proj_in, 5, 8, sums)
    features_end(sums, proj_out, live, fp, block)

    def begin():
        for copy in first:
            copy.start()

    events = sorted([(times[n], n) for n in range(len(msgs))]
                    + [(BEGIN_AT, -4), (SUM_AT, -1), (SPREAD_AT, -2), (PANEL_AT, -3)])
    for _, n in events:
        if n < 0:
            (sum_up, spread, panel, begin)[-n - 1]()
            continue
        darrived(n)
        for f, m in enumerate(msgs):
            if m.dep is msgs[n]:
                dcopy(f).start()
    for i in range(NY):
        off = here if i == 0 else neg(y_off[i - 1])
        there = take_of(add(off, core))
        rdma(there, there, s4.at[i], r4.at[i], device(me, core)).wait_recv()
    for n in range(len(msgs)):
        dcopy(n).wait_send()
    for copy in first + second + third:
        copy.wait_send()
    for e in range(2):
        @pl.when(jnp.logical_not(at_home[e]))
        def _():
            leg[e].wait_send()
    for i in range(NY):
        give(i).wait_send()
    kept.wait()


def features_part(tok, cot, wts, proj_in, lo, hi, sums):
    f32 = jnp.float32
    rows, step = tok.shape[0], 512

    def body(i, acc):
        cs = pl.ds(pl.multiple_of(i * step, step), step)
        t = tok[:, cs]
        g, h, p = acc
        return (g + jnp.dot(t, wts[cs, :512], preferred_element_type=f32),
                h + jnp.dot(cot[:, cs], wts[cs, 384:], preferred_element_type=f32),
                p + jnp.dot(t, proj_in[cs, :], preferred_element_type=f32))
    if sums is None:
        sums = (jnp.zeros((rows, 512), f32), jnp.zeros((rows, 512), f32), jnp.zeros((rows, 128), f32))
    return lax.fori_loop(lo, hi, body, sums)


def features_end(sums, proj_out, live, fp, block):
    f32 = jnp.float32
    hidden = 448
    g, h, p = sums
    h = pltpu.roll(h, 512 - 64, 1)
    lane = lax.broadcasted_iota(jnp.int32, h.shape, 1)
    up = jnp.where(lane < hidden, h * (g / (1.0 + jnp.exp(-g))), 0.0).astype(jnp.bfloat16)
    outer = jnp.dot(up, proj_out[...], preferred_element_type=f32)
    p = p * live[...]
    for s in range(2):
        total = jnp.zeros((128, 128), f32)
        for e in range(2):
            ts = slice((2 * s + e) * 64, (2 * s + e + 1) * 64)
            o = outer[ts] if e == 0 else pltpu.roll(outer[ts], 64, 1)
            total = total + tdot(p[ts], o, HI)
        block[...] = total
        for c in range(16):
            fp[c, pl.ds(8 * s, 8), :] = block[pl.ds(c, 8, stride=16), :]


def exchange(tok, cot, wts, proj_in, proj_out, live, gp, head):
    band, wide = head.shape[0], HALF + head.shape[1]
    msgs = exchange_messages(band * wide * 2)
    times = ordered(msgs)
    vm = pl.BlockSpec(memory_space=pltpu.VMEM)
    f32 = jnp.float32
    rows, cols = NZ * NX, NY * NC
    dma = pltpu.SemaphoreType.DMA

    def body(*refs):
        exchange_kernel(msgs, times, *refs)
    return pl.pallas_call(
        body,
        out_shape=(
            jax.ShapeDtypeStruct((rows * 16, 128), f32),
            jax.ShapeDtypeStruct((cols * TAKE, 128), f32),
            jax.ShapeDtypeStruct((rows * band, wide), f32),
            jax.ShapeDtypeStruct((rows * band, HALF), f32)),
        in_specs=[vm] * 8, out_specs=(vm,) * 4,
        scratch_shapes=[
            pltpu.VMEM((cols, 16, 128), f32), pltpu.VMEM((band, wide), f32), pltpu.VMEM((128, 128), f32),
            pltpu.VMEM((cols - 1, 16, 128), f32), pltpu.VMEM((16, 128), f32), pltpu.VMEM((TAKE, 128), f32),
            dma((len(msgs),)), dma((len(msgs),)), dma((cols - 1,)), dma((cols - 1,)), dma((rows - 1,)), dma((rows - 1,)),
            dma((2,)), dma((2,)), dma((NY - 1,)), dma((NY - 1,)), dma((NY,)), dma((NY,)), dma],
        compiler_params=pltpu.CompilerParams(collective_id=1, has_side_effects=True, vmem_limit_bytes=14 << 20),
        name="exchange",
    )(tok, cot, wts, proj_in, proj_out, live, gp, head)


def lanes(x, j):
    return jnp.broadcast_to(x[:, j:j + 1], x.shape)


def subl(x, k):
    return jnp.broadcast_to(x[k:k + 1, :], x.shape)


def factor_block(A, V, group=8):
    n = len(A)
    A, V = list(A), list(V)
    sub = lax.broadcasted_iota(jnp.int32, (8, NB), 0)
    for g in range(0, n, group):
        for p in range(g, g + group):
            a, v = A[p], V[p]
            C = [lanes(a, 8 * p + j) for j in range(8)]
            Us, Vs, R, S = [], [], [], []
            for k in range(8):
                r = lax.rsqrt(subl(C[k], k))
                sb = [subl(C[k], j) if j > k else None for j in range(8)]
                Cs = C[k] * (r * r)
                for j in range(k + 1, 8):
                    C[j] = C[j] - Cs * sb[j]
                R.append(r)
                S.append([None if t is None else t * r for t in sb])
                uk, vk = subl(a, k) * r, subl(v, k) * r
                m = jnp.where(sub > k, C[k] * r, 0.0)
                a, v = a - m * uk, v - m * vk
                Us.append(uk)
                Vs.append(vk)
            un, vn = Us[0], Vs[0]
            for k in range(1, 8):
                un = jnp.where(sub == k, Us[k], un)
                vn = jnp.where(sub == k, Vs[k], vn)
            A[p], V[p] = un, vn
            for q in range(p + 1, g + group):
                aq, vq = A[q], V[q]
                G = [lanes(aq, 8 * p + j) for j in range(8)]
                L = []
                for k in range(8):
                    t = G[k]
                    for m in range(k):
                        t = t - L[m] * S[m][k]
                    L.append(t * R[k])
                for k in range(8):
                    aq, vq = aq - L[k] * Us[k], vq - L[k] * Vs[k]
                A[q], V[q] = aq, vq
        if g + group < n:
            ug = jnp.concatenate(A[g:g + group], 0)
            vg = jnp.concatenate(V[g:g + group], 0)
            change = tdot(ug, jnp.concatenate([ug, vg], 1), HI)
            for q in range(g + group, n):
                A[q] = A[q] - change[8 * q:8 * q + 8, :NB]
                V[q] = V[q] - change[8 * q:8 * q + 8, NB:]
    return A, V


def split3(x):
    h = x.astype(jnp.bfloat16)
    rest = x - h.astype(jnp.float32)
    m = rest.astype(jnp.bfloat16)
    return h, m, (rest - m.astype(jnp.float32)).astype(jnp.bfloat16)


def tdot(a, b, precision=None):
    return lax.dot_general(a, b, (((0,), (0,)), ((), ())), precision=precision, preferred_element_type=jnp.float32)


def paired(even, odd, lane):
    return jnp.where(lane < 64, even, pltpu.roll(odd, 64, 1)), jnp.where(lane < 64, pltpu.roll(even, 64, 1), odd)


def factor_kernel(x, y, gp, all3, col_all, upd, both, strip, own, u, inv, hh, hm, ml, mh, rowp, frow, fcol):
    n, width = u.shape
    nb, half = n // NB, n // 2
    r, c = lax.axis_index("rows"), lax.axis_index("cols")
    k = lax.rem(c, NC)
    cols = NY * NC
    seqs = 128
    per = seqs // (NZ * NX)
    heads = 16
    lane64 = lax.broadcasted_iota(jnp.int32, (64, NB), 1)

    def keep(h, m, l, cs):
        hh[pl.ds(0, NB), cs] = h
        hh[pl.ds(NB, NB), cs] = h
        hm[pl.ds(0, NB), cs] = h
        hm[pl.ds(NB, NB), cs] = m
        ml[pl.ds(0, NB), cs] = m
        ml[pl.ds(NB, NB), cs] = l
        mh[pl.ds(0, NB), cs] = m
        mh[pl.ds(NB, NB), cs] = h

    def product(qs, cs):
        return tdot(hh[:, qs], hm[:, cs]) + (tdot(ml[:, qs], hh[:, cs]) + tdot(mh[:, qs], ml[:, cs]))

    for p in range(cols // 2):
        top, low = paired(all3[pl.ds(2 * p * TAKE, 64), :], all3[pl.ds((2 * p + 1) * TAKE, 64), :], lane64)
        keep(*split3(jnp.concatenate([top, low], 0)), pl.ds(p * NB, NB))
    for p in range(cols):
        rowp[pl.ds(32 * p, 32), :] = all3[pl.ds(p * TAKE + 64, 32), :]
    for p in range(4):
        top, low = paired(col_all[pl.ds(2 * p, 64, stride=8), :], col_all[pl.ds(2 * p + 1, 64, stride=8), :], lane64)
        fcol[pl.ds(0, 64), pl.ds(p * NB, NB)] = top
        fcol[pl.ds(64, 64), pl.ds(p * NB, NB)] = low
    second = lax.rem(r, 2) == 1
    for t in range(2):
        top = low = jnp.zeros((64, NB), jnp.float32)
        for q in range(4):
            piece = rowp[pl.ds(4 * t + q, 64, stride=8), :]
            piece = jnp.where(second, pltpu.roll(piece, 96, 1), piece)
            here = lane64 // 32 == q
            top = jnp.where(here, piece if q == 0 else pltpu.roll(piece, 32 * q, 1), top)
            low = jnp.where(here, piece if q == 2 else pltpu.roll(piece, (32 * q + 64) % 128, 1), low)
        frow[pl.ds(0, 64), pl.ds(t * NB, NB)] = top
        frow[pl.ds(64, 64), pl.ds(t * NB, NB)] = low
    at = lax.broadcasted_iota(jnp.int32, (seqs, NB), 0)
    lane = lax.broadcasted_iota(jnp.int32, (seqs, NB), 1)
    seq = 2 * (at - jnp.where(at >= 64, 64, 0)) + jnp.where(at >= 64, 1, 0)
    wanted = jnp.logical_and(jnp.logical_and(lane >= heads, lane < heads + per), seq == per * r + lane - heads)
    pick = jnp.where(wanted, jnp.float32(seqs), 0.0)
    keep(*split3(jnp.where(lane < 32, pick, frow[:, :NB])), pl.ds(n, NB))
    keep(*split3(frow[:, NB:]), pl.ds(n + NB, NB))
    upd[...] = tdot(frow[...], fcol[...], HI) * (1.0 / seqs)

    for b in range(nb):
        rows = pl.ds(b * NB, NB)
        u[rows, pl.ds(pl.multiple_of(k * HALF, HALF), HALF)] = x[rows, :HALF]
        u[rows, pl.ds(pl.multiple_of((1 - k) * HALF, HALF), HALF)] = y[rows, :]
        u[rows, n:n + NB] = jnp.where(lane < heads, x[rows, HALF:], jnp.where(lane < 32, 0.0, gp[rows, :NB]))
        u[rows, n + NB:] = gp[rows, NB:]
        cs = pl.ds(b * NB, width - b * NB)
        u[rows, cs] = u[rows, cs] + product(rows, cs) * (1.0 / seqs)

    row = lax.broadcasted_iota(jnp.int32, (8, NB), 0)
    col = lax.broadcasted_iota(jnp.int32, (8, NB), 1)

    def outer(b, _):
        o = pl.multiple_of(b * NB, NB)
        rows = pl.ds(o, NB)
        A = [u[pl.ds(o + 8 * p, 8), rows] for p in range(NB // 8)]
        V = [jnp.where(col == row + 8 * p, 1.0, 0.0) for p in range(NB // 8)]
        A, V = factor_block(A, V)
        for p in range(NB // 8):
            inv[pl.ds(8 * p, 8), :] = V[p]
        ih, im, il = split3(inv[...])
        hh_l, ml_l, mh_l = (jnp.concatenate(pair, 1) for pair in ((ih, ih), (im, il), (im, ih)))

        def dot(a, top, low):
            return jnp.dot(a, jnp.concatenate([top, low], 0), preferred_element_type=jnp.float32)

        def scale(lo, hi):
            for t in range(lo, hi, 256):
                cs = pl.ds(t, 256)
                h, m, l = split3(u[rows, cs])
                new = dot(hh_l, h, m) + (dot(ml_l, h, h) + dot(mh_l, m, l))
                u[rows, cs] = new
                keep(*split3(new), cs)

        @pl.when(b < nb // 2)
        def _():
            scale(0, half)
        scale(half, width)
        for p in range(NB // 8):
            u[pl.ds(o + 8 * p, 8), rows] = jnp.where(col >= row + 8 * p, A[p], 0.0)

        def trail(lo):
            def body(q, _):
                qs = pl.ds(pl.multiple_of(q * NB, NB), NB)
                cs = pl.ds(lo, width - lo)
                u[qs, cs] = u[qs, cs] - product(qs, cs)
                return 0
            return body
        lax.fori_loop(b + 1, nb // 2, trail(0), 0)
        lax.fori_loop(jnp.maximum(b + 1, nb // 2), nb, trail(half), 0)
        return 0
    lax.fori_loop(0, nb, outer, 0)

    extra = pl.ds(n, width - n)
    both[...] = tdot(u[:, n:n + NB], u[:, n:], HI)[:heads]
    own[...] = u[pl.ds(pl.multiple_of(32 * r, 32), 32), n:n + NB]
    mine = pl.ds(pl.multiple_of(64 * c, 64), 64)
    tile = pltpu.roll(u[mine, pl.ds(pl.multiple_of((r // 4) * NB, NB), NB)], lax.rem(128 - 32 * lax.rem(r, 4), 128), 1)
    down = lax.broadcasted_iota(jnp.int32, (64, NB), 0) + 64 * c
    tile = jnp.where(lane64 + 32 * r >= down, tile, 0.0)
    strip[:, :NB] = jnp.where(lane64 < 32, tile, u[mine, n:n + NB])
    strip[:, NB:] = u[mine, n + NB:]


def factored(x, y, gp, all3, col_all):
    n, f32 = x.shape[0], jnp.float32
    vm = pl.BlockSpec(memory_space=pltpu.VMEM)
    packed = pltpu.VMEM((2 * NB, n + 256), jnp.bfloat16)
    return pl.pallas_call(
        factor_kernel,
        out_shape=(
            jax.ShapeDtypeStruct((256, 512), f32), jax.ShapeDtypeStruct((16, 256), f32),
            jax.ShapeDtypeStruct((64, 256), f32), jax.ShapeDtypeStruct((32, 128), f32)),
        in_specs=[vm] * 5, out_specs=(vm,) * 4,
        scratch_shapes=[
            pltpu.VMEM((n, n + 256), f32), pltpu.VMEM((NB, NB), f32), packed, packed, packed, packed,
            pltpu.VMEM((512, NB), f32), pltpu.VMEM((NB, 256), f32), pltpu.VMEM((NB, 512), f32)],
        compiler_params=pltpu.CompilerParams(vmem_limit_bytes=20 << 20),
        name="factor",
    )(x, y, gp, all3, col_all)


def local(tokens, cotangent, gate_weight, down_weight, proj_in, proj_out, lengths, loss_mask, gram_in, queries):
    f32 = jnp.float32
    cycles, band_rows, _, band_cols = gram_in.shape
    seq_count, window = loss_mask.shape

    weights = jnp.concatenate([gate_weight, down_weight], axis=1)
    band = gram_in[:, :, 0, :].reshape(cycles * band_rows, band_cols).T
    positions = jnp.arange(window, dtype=jnp.int32)
    live = (positions[None, :] >= (window - lengths)[:, None]).astype(f32) * loss_mask.astype(f32)
    outer_in = jnp.pad(proj_out, ((0, 512 - proj_out.shape[0]), (0, 128 - proj_out.shape[1])))
    live = jnp.broadcast_to(live.reshape(seq_count * window, 1), (seq_count * window, proj_in.shape[1]))
    head = jnp.pad(queries[:, 0, :].T, ((0, 0), (0, 128 - queries.shape[0])))
    weights, band, outer_in, live, head = lax.optimization_barrier((weights, band, outer_in, live, head))
    tok, cot, wts, gp = gather(tokens, cotangent, weights, band)

    col_all, all3, d_own, d_other = exchange(tok, cot, wts, proj_in, outer_in, live, gp, head)
    upd, both, strip, own = factored(d_own, d_other, gp, all3, col_all)

    panel = strip.T.reshape(cycles, band_rows, 1, band_cols)
    which = lax.broadcasted_iota(jnp.int32, gram_in.shape, 2)
    gram_next = jnp.where(which == 0, panel, gram_in + upd.reshape(gram_in.shape))
    count = queries.shape[0]
    scores = both[:, count:count + seq_count]
    tail = queries[:, 1:] - both[:, band_rows:].reshape(count, cycles - 1, band_rows)
    query_next = jnp.concatenate([own[:, :count].T[:, None], tail], axis=1)
    return gram_next, query_next, scores


def solution(mesh):
    return jax.shard_map(
        local,
        mesh=mesh,
        in_specs=(
            P("rows", "cols"), P("rows", "cols"), P("rows", "cols"), P("rows", "cols"), P(), P("cols", None),
            P("rows"), P("rows", None), P(None, "rows", None, "cols"), P("cols", None, "rows")),
        out_specs=(P(None, "rows", None, "cols"), P("cols", None, "rows"), P("cols", "rows")),
        check_vma=False,
    )
```
